512 devices in a mesh: gx: 64 (over z, x_hi, core), gy: 8 (over x_lo, y).
Axes of the slice: x: 4 (x_hi: 2, x_lo: 2; x = x_hi * 2 + x_lo), y: 4, z: 16, core: 2. Of those that a mesh axis runs over, the one named last changes fastest.
Arguments:
- initial: float32 [256, 1024, 512], P('gx', 'gy'), may hold values from -4 to 4
- kappa: float32 [256, 1024, 512], P('gx', 'gy'), may hold values from 0.04 to 0.12
- velocity: float32 [256, 1024, 512], P('gx', 'gy'), may hold values from 0.05 to 0.2
- rate: float32 [256, 1024, 512], P('gx', 'gy'), may hold values from 0.05 to 0.3
Outputs:
- final: float32 [256, 1024, 512], P('gx', 'gy')
The draws below stay inside these ranges and needn't reach their ends.
All inputs are finite; a program needn't handle non-finite values.
Results may differ from the reference program's by a relative error of at most 0.00002.
Values sent between devices are 32-bit elements; how exact they have to be, the bound alone decides.
A program may use at most 64 MiB of HBM per device.

```python
import math
import jax
import jax.numpy as jnp

CX = 4
CZ = 512
STEPS = 4
ITERS = 2
NX = 256
NY = 1024
N_GX = 64


def level_of(key, extent, split, smallest, top_value):
    def one(axis_at, parts):
        heights = jax.random.uniform(jax.random.fold_in(jax.random.fold_in(key, 6), axis_at), (parts,), jnp.float32, smallest / len(split), top_value / len(split))
        return jnp.repeat(jnp.exp(heights), extent[axis_at] // parts).reshape((-1,) + (1,) * (len(extent) - axis_at - 1))

    level = one(*split[0])
    for cut in split[1:]:
        level = level * one(*cut)
    return level


def gaussian(rng, extent, spread, most, cuts=(), held_as=jnp.bfloat16):
    drawn = jax.random.normal(rng, extent, jnp.float32) * spread
    if len(cuts) > 0:
        drawn = level_of(rng, extent, cuts, -0.22, 0.18) * drawn
    return jnp.clip(drawn, min=-most, max=most).astype(held_as)


def setup_inputs(seed: int = 0) -> dict:
    key_of = jax.random.split(jax.random.key(seed), 5)
    return {
        "initial": gaussian(key_of[0], (NX, NY, CZ), 1.0, 4.0, ((0, 64), (1, 8)), jnp.float32),
        "kappa": jnp.clip(0.04 + 0.08 * jax.random.uniform(key_of[1], (NX, NY, CZ), jnp.float32) ** level_of(key_of[1], (NX, NY, CZ), ((0, 64), (1, 8)), -0.2, 0.2), 0.04, 0.12),
        "velocity": jnp.clip(0.05 + 0.15 * jax.random.uniform(key_of[2], (NX, NY, CZ), jnp.float32) ** level_of(key_of[2], (NX, NY, CZ), ((0, 64), (1, 8)), -0.2, 0.2), 0.05, 0.2),
        "rate": jnp.clip(jnp.exp(math.log(0.3) - 1.7917595 * jax.random.uniform(key_of[3], (NX, NY, CZ), jnp.float32) ** level_of(key_of[3], (NX, NY, CZ), ((0, 64), (1, 8)), -0.2, 0.2)), 0.05, 0.3),
    }


robin_p = 0.6


def advance(field, kappa, velocity, rate, data_left, data_right):
    first = field[:, 0]
    last = field[:, -1]
    ghost_left = (data_left + first * (1.0 - robin_p / 2)) / (1.0 + robin_p / 2)
    ghost_right = (data_right + last * (1.0 - robin_p / 2)) / (1.0 + robin_p / 2)
    extended = jnp.concatenate([ghost_left[:, None], field, ghost_right[:, None]], axis=1)
    extended = jnp.pad(extended, ((0, 0), (0, 0), (1, 1), (1, 1)))
    center = extended[:, 1:-1, 1:-1, 1:-1]
    minus_x = extended[:, :-2, 1:-1, 1:-1]
    lap = extended[:, 2:, 1:-1, 1:-1] + minus_x
    lap = lap + extended[:, 1:-1, 2:, 1:-1] + extended[:, 1:-1, :-2, 1:-1]
    lap = lap + extended[:, 1:-1, 1:-1, 2:] + extended[:, 1:-1, 1:-1, :-2]
    lap = lap - 6.0 * center
    react = rate * center ** 3 / (1.0 + center * center)
    updated = center + kappa * lap - velocity * (center - minus_x) - react
    return updated, first, ghost_left, last, ghost_right


def reference(initial, kappa, velocity, rate):
    shape = (N_GX, CX, NY, CZ)
    start = initial.reshape(shape)
    kappa_s = kappa.reshape(shape)
    velocity_s = velocity.reshape(shape)
    rate_s = rate.reshape(shape)
    zero_plane = jnp.zeros((N_GX, NY, CZ), jnp.float32)
    data_left = [zero_plane] * STEPS
    data_right = [zero_plane] * STEPS
    field = start
    for sweep in range(ITERS):
        field = start
        traces = []
        for step in range(STEPS):
            field, first, ghost_left, last, ghost_right = advance(field, kappa_s, velocity_s, rate_s, data_left[step], data_right[step])
            traces.append((first, ghost_left, last, ghost_right))
        if sweep + 1 < ITERS:
            new_left = []
            new_right = []
            for step in range(STEPS):
                first, ghost_left, last, ghost_right = traces[step]
                toward_prev = (first - ghost_left) + robin_p * (first + ghost_left) / 2
                toward_next = (last - ghost_right) + robin_p * (last + ghost_right) / 2
                new_right.append(jnp.roll(toward_prev, -1, axis=0))
                new_left.append(jnp.roll(toward_next, 1, axis=0))
            data_left = new_left
            data_right = new_right
    return field.reshape(NX, NY, CZ)
```

```python
import functools

import jax
import jax.numpy as jnp
from jax import lax
from jax.experimental import pallas as pl
from jax.experimental.pallas import tpu as pltpu
from jax.sharding import PartitionSpec as P

STEPS = 4
robin_p = 0.6
MESH = pl.DeviceIdType.MESH
FACE_W = (1.0 - robin_p / 2) / (1.0 + robin_p / 2)
SENT_W = (1.0 - FACE_W) + robin_p * (1.0 + FACE_W) / 2
DATA_W = SENT_W / (1.0 + robin_p / 2)
NB = 4
ROWS = 128
TOP = 8


def places():
    gx, gy = lax.axis_index("gx"), lax.axis_index("gy")
    ngx = lax.axis_size("gx")
    core = gx % 2
    x = ((gx // 2) % 2) * 2 + gy // 4

    def chip(step):
        other = (x + step + 4) % 4
        return ((gx // 4) * 4 + (other // 2) * 2 + core, (other % 2) * 4 + gy % 4)

    def target(of):
        return ((of[0] + 2 * core - 1 + ngx) % ngx, of[1])

    source_gx = (gx - 1 + 2 * core + ngx) % ngx
    source_x = ((source_gx // 2) % 2) * 2 + gy // 4

    def source_relay(step):
        other = (source_x + step + 4) % 4
        return (
            (source_gx // 4) * 4 + (other // 2) * 2 + source_gx % 2,
            (other % 2) * 4 + gy % 4,
        )

    plus, minus = chip(1), chip(-1)
    return dict(
        core=core,
        gy=gy,
        partner=(gx + 1 - 2 * core, gy),
        plus=plus,
        minus=minus,
        target_of_minus=target(minus),
        target_of_plus=target(plus),
        deliver_a=source_relay(1),
        deliver_b=source_relay(-1),
        up=(gx, gy - 1),
        down=(gx, gy + 1),
    )


def kernel(
    init, kap, vel, rat, out,
    u0, u1, u2, u3, v1, v2, v3, o4, kb, vb, rb, ab, got, relay, stage, halo,
    load_sem, out_sem, near_s, near_r, far_s, far_r, hop_s, hop_r, edge_s, edge_r,
):
    here = places()
    core, gy = here["core"], here["gy"]
    last_gy = lax.axis_size("gy") - 1

    loads = []
    for at, (hbm, vmem, top) in enumerate(
        ((init, u0, TOP), (kap, kb, 0), (vel, vb, 0), (rat, rb, 0))
    ):
        for k in range(NB):
            copy = pltpu.make_async_copy(
                hbm.at[:, :, 128 * k : 128 * (k + 1)],
                vmem.at[:, k, top : top + ROWS, :],
                load_sem.at[at * NB + k],
            )
            copy.start()
            loads.append(copy)

    barrier = pltpu.get_barrier_semaphore()
    for who in ("partner", "plus", "minus", "deliver_a", "deliver_b"):
        pl.semaphore_signal(barrier, inc=1, device_id=here[who], device_id_type=MESH)

    @pl.when(gy > 0)
    def _():
        pl.semaphore_signal(barrier, inc=1, device_id=here["up"], device_id_type=MESH)

    @pl.when(gy < last_gy)
    def _():
        pl.semaphore_signal(barrier, inc=1, device_id=here["down"], device_id_type=MESH)

    @pl.when(gy == 0)
    def _():
        for e in range(6):
            halo[e, 0] = jnp.zeros((16, 128), jnp.float32)

    @pl.when(gy == last_gy)
    def _():
        for e in range(6):
            halo[e, 1] = jnp.zeros((16, 128), jnp.float32)

    edges = jnp.where(gy > 0, 1, 0) + jnp.where(gy < last_gy, 1, 0)
    pl.semaphore_wait(barrier, 5 + edges)

    def remote(src, dst, send, recv, who):
        return pltpu.make_async_remote_copy(
            src_ref=src, dst_ref=dst, send_sem=send, recv_sem=recv,
            device_id=here[who], device_id_type=MESH,
        )

    def near_copy(n, ref, top, stride):
        return remote(
            ref.at[(1 - core) * stride, :, top : top + ROWS, :],
            got.at[core, n], near_s.at[n], near_r.at[n], "partner",
        )

    def far_copy(n, ref, top, stride, way):
        return remote(
            ref.at[core * stride, 2 * way : 2 * way + 2, top : top + ROWS, :],
            relay.at[n, way], far_s.at[n, way], hop_r.at[n, way],
            "minus" if way else "plus",
        )

    def hop_copy(n, way):
        return remote(
            relay.at[n, way], got.at[1 - core, n, 2 * way : 2 * way + 2],
            hop_s.at[n, way], far_r.at[n, way],
            "target_of_plus" if way else "target_of_minus",
        )

    sends = []

    def send_faces(n, ref, top, stride):
        for way in range(2):
            copy = far_copy(n, ref, top, stride, way)
            copy.start()
            sends.append(copy)
        copy = near_copy(n, ref, top, stride)
        copy.start()
        sends.append(copy)

    def relay_on(n):
        for way in range(2):
            far_copy(n, u0, TOP, 3, way).wait_recv()
            copy = hop_copy(n, way)
            copy.start()
            sends.append(copy)

    def wait_faces(n):
        near_copy(n, u0, TOP, 3).wait_recv()
        for way in range(2):
            hop_copy(n, way).wait_recv()

    def edge_copies(e):
        up = remote(stage.at[e, 0], halo.at[e, 1], edge_s.at[e, 0], edge_r.at[e, 1], "up")
        down = remote(stage.at[e, 1], halo.at[e, 0], edge_s.at[e, 1], edge_r.at[e, 0], "down")
        return up, down

    def send_edges(e, planes):
        for p, (ref, i) in enumerate(planes):
            for k in range(NB):
                at = p * NB + k
                stage[e, 0, at : at + 1, :] = ref[i, k, TOP : TOP + 1, :]
                stage[e, 1, at : at + 1, :] = ref[i, k, TOP + ROWS - 1 : TOP + ROWS, :]
        up, down = edge_copies(e)

        @pl.when(gy > 0)
        def _():
            up.start()

        @pl.when(gy < last_gy)
        def _():
            down.start()

    def take_edges(e, planes):
        up, down = edge_copies(e)

        @pl.when(gy > 0)
        def _():
            down.wait_recv()

        @pl.when(gy < last_gy)
        def _():
            up.wait_recv()

        for p, (ref, i) in enumerate(planes):
            for k in range(NB):
                at = p * NB + k
                ref[i, k, TOP - 1 : TOP, :] = halo[e, 0, at : at + 1, :]
                ref[i, k, TOP + ROWS : TOP + ROWS + 1, :] = halo[e, 1, at : at + 1, :]

    lane = lax.broadcasted_iota(jnp.int32, (NB, 8, 128), 2)
    at_first, at_last = lane == 0, lane == 127
    zero = jnp.zeros((1, 8, 128), jnp.float32)

    def step(planes, which, dest, dest_top, data=None, fresh=False):
        def body(r, carry):
            row = pl.multiple_of(r * 8, 8)

            def read(p, shift=0):
                ref, i = planes[p]
                return ref[i, :, pl.ds(row + TOP + shift, 8), :]

            need = sorted({q for p in which for q in (p - 1, p, p + 1) if 0 <= q < 4})
            cells = {p: read(p) for p in need}

            def ghost(side, face):
                if data is None:
                    return face * FACE_W
                return face * FACE_W + got[side, data, :, pl.ds(row, 8), :] * DATA_W

            for p in which:
                c = cells[p]
                minus_x = cells[p - 1] if p > 0 else ghost(0, c)
                plus_x = cells[p + 1] if p < 3 else ghost(1, c)
                ahead, behind = pltpu.roll(c, 127, 2), pltpu.roll(c, 1, 2)
                plus_z = jnp.where(at_last, jnp.concatenate([ahead[1:], zero], 0), ahead)
                minus_z = jnp.where(at_first, jnp.concatenate([zero, behind[:-1]], 0), behind)
                total = (plus_x + minus_x) + (read(p, 1) + read(p, -1)) + (plus_z + minus_z)
                k = kb[p, :, pl.ds(row, 8), :]
                v = vb[p, :, pl.ds(row, 8), :]
                q = rb[p, :, pl.ds(row, 8), :]
                if fresh:
                    a = (1.0 - 6.0 * k) - (v + q)
                    ab[p, :, pl.ds(row, 8), :] = a
                else:
                    a = ab[p, :, pl.ds(row, 8), :]
                inner = a + q * pl.reciprocal(1.0 + c * c)
                ref, i = dest[p]
                ref[i, :, pl.ds(row + dest_top, 8), :] = c * inner + (k * total + v * minus_x)
            return carry

        lax.fori_loop(0, ROWS // 8, body, 0)

    def whole(ref):
        return [(ref, p) for p in range(4)]

    a0, a1, a2 = whole(u0), whole(u1), whole(u2)
    a3 = {0: (u3, 0), 3: (u3, 1)}
    b1 = [(v1, 0), (u1, 1), (u1, 2), (v1, 1)]
    b1_edges = [(v1, 0), (v1, 1)]
    b2, b3, b4 = whole(v2), whole(v3), whole(o4)
    outer, inner = (0, 3), (1, 2)

    for copy in loads[:NB]:
        copy.wait()
    send_edges(0, a0)
    send_faces(0, u0, TOP, 3)
    for copy in loads[NB:]:
        copy.wait()
    take_edges(0, a0)
    step(a0, outer, a1, TOP, fresh=True)
    send_faces(1, u1, TOP, 3)
    step(a0, inner, a1, TOP, fresh=True)
    send_edges(1, a1)
    relay_on(0)
    take_edges(1, a1)
    step(a1, outer, a2, TOP)
    send_faces(2, u2, TOP, 3)
    step(a1, inner, a2, TOP)
    send_edges(2, a2)
    take_edges(2, a2)
    step(a2, outer, a3, 0)
    send_faces(3, u3, 0, 1)
    relay_on(1)
    wait_faces(0)
    step(a0, outer, {0: b1[0], 3: b1[3]}, TOP, data=0)
    send_edges(3, b1_edges)
    relay_on(2)
    step(b1, inner, b2, TOP)
    take_edges(3, b1_edges)
    wait_faces(1)
    step(b1, outer, b2, TOP, data=1)
    send_edges(4, b2)
    relay_on(3)
    take_edges(4, b2)
    step(b2, inner, b3, TOP)
    wait_faces(2)
    step(b2, outer, b3, TOP, data=2)
    send_edges(5, b3)
    take_edges(5, b3)
    step(b3, inner, b4, 0)

    def put(first, count, at):
        copies = []
        for k in range(NB):
            copy = pltpu.make_async_copy(
                o4.at[first : first + count, k],
                out.at[first : first + count, :, 128 * k : 128 * (k + 1)],
                out_sem.at[at * NB + k],
            )
            copy.start()
            copies.append(copy)
        return copies

    puts = put(1, 2, 0)
    wait_faces(3)
    step(b3, outer, b4, 0, data=3)
    puts += put(0, 1, 1) + put(3, 1, 2)
    for copy in sends:
        copy.wait_send()
    for e in range(6):
        up, down = edge_copies(e)

        @pl.when(gy > 0)
        def _():
            up.wait_send()

        @pl.when(gy < last_gy)
        def _():
            down.wait_send()

    for copy in puts:
        copy.wait()


def local(initial, kappa, velocity, rate):
    haloed, plain = (4, NB, ROWS + 16, 128), (4, NB, ROWS, 128)
    f32 = lambda *shape: pltpu.VMEM(shape, jnp.float32)
    dma = pltpu.SemaphoreType.DMA
    return pl.pallas_call(
        kernel,
        out_shape=jax.ShapeDtypeStruct(initial.shape, jnp.float32),
        in_specs=[pl.BlockSpec(memory_space=pl.ANY)] * 4,
        out_specs=pl.BlockSpec(memory_space=pl.ANY),
        scratch_shapes=[
            f32(*haloed), f32(*haloed), f32(*haloed), f32(2, NB, ROWS, 128),
            f32(2, NB, ROWS + 16, 128), f32(*haloed), f32(*haloed), f32(*plain),
            f32(*plain), f32(*plain), f32(*plain), f32(*plain),
            f32(2, STEPS, NB, ROWS, 128), f32(STEPS, 2, 2, ROWS, 128),
            f32(6, 2, 16, 128), f32(6, 2, 16, 128),
            dma((16,)), dma((12,)), dma((STEPS,)), dma((STEPS,)),
            dma((STEPS, 2)), dma((STEPS, 2)), dma((STEPS, 2)), dma((STEPS, 2)),
            dma((6, 2)), dma((6, 2)),
        ],
        compiler_params=pltpu.CompilerParams(collective_id=0, has_side_effects=True),
        name="window",
    )(initial, kappa, velocity, rate)


def solution(mesh):
    placed = P("gx", "gy", None)
    return jax.shard_map(
        local, mesh=mesh, in_specs=(placed,) * 4, out_specs=placed, check_vma=False
    )
```

```python
import jax
import jax.numpy as jnp
from jax import lax
from jax.experimental import pallas as pl
from jax.experimental.pallas import tpu as pltpu
from jax.sharding import PartitionSpec as P

STEPS = 4
robin_p = 0.6
MESH = pl.DeviceIdType.MESH
FACE_W = (1.0 - robin_p / 2) / (1.0 + robin_p / 2)
SENT_W = (1.0 - FACE_W) + robin_p * (1.0 + FACE_W) / 2
DATA_W = SENT_W / (1.0 + robin_p / 2)
NB = 4
ROWS = 128
TOP = 8
MARGIN = 4


def places():
    gx, gy = lax.axis_index("gx"), lax.axis_index("gy")
    ngx = lax.axis_size("gx")
    core = gx % 2
    x = ((gx // 2) % 2) * 2 + gy // 4

    def chip(step):
        other = (x + step + 4) % 4
        return ((gx // 4) * 4 + (other // 2) * 2 + core, (other % 2) * 4 + gy % 4)

    def target(of):
        return ((of[0] + 2 * core - 1 + ngx) % ngx, of[1])

    source_gx = (gx - 1 + 2 * core + ngx) % ngx
    source_x = ((source_gx // 2) % 2) * 2 + gy // 4

    def source_relay(step):
        other = (source_x + step + 4) % 4
        return (
            (source_gx // 4) * 4 + (other // 2) * 2 + source_gx % 2,
            (other % 2) * 4 + gy % 4,
        )

    plus, minus = chip(1), chip(-1)
    return dict(
        core=core,
        gy=gy,
        partner=(gx + 1 - 2 * core, gy),
        plus=plus,
        minus=minus,
        target_of_minus=target(minus),
        target_of_plus=target(plus),
        deliver_a=source_relay(1),
        deliver_b=source_relay(-1),
        up=(gx, gy - 1),
        down=(gx, gy + 1),
    )


def kernel(
    init, kap, vel, rat, out,
    u0, u1, u2, u3, v1, v2, v3, o4, kb, vb, rb, ab, got, relay,
    load_sem, out_sem, near_s, near_r, far_s, far_r, hop_s, hop_r, edge_s, edge_r,
):
    here = places()
    core, gy = here["core"], here["gy"]
    last_gy = lax.axis_size("gy") - 1
    arrays = ((init, u0), (kap, kb), (vel, vb), (rat, rb))

    loads = []
    for at, (hbm, vmem) in enumerate(arrays):
        for k in range(NB):
            copy = pltpu.make_async_copy(
                hbm.at[:, :, 128 * k : 128 * (k + 1)],
                vmem.at[:, k, TOP : TOP + ROWS, :],
                load_sem.at[at * NB + k],
            )
            copy.start()
            loads.append(copy)

    barrier = pltpu.get_barrier_semaphore()
    for who in ("partner", "plus", "minus", "deliver_a", "deliver_b"):
        pl.semaphore_signal(barrier, inc=1, device_id=here[who], device_id_type=MESH)

    @pl.when(gy > 0)
    def _():
        pl.semaphore_signal(barrier, inc=1, device_id=here["up"], device_id_type=MESH)

    @pl.when(gy < last_gy)
    def _():
        pl.semaphore_signal(barrier, inc=1, device_id=here["down"], device_id_type=MESH)

    @pl.when(gy == 0)
    def _():
        for _, vmem in arrays:
            vmem[:, :, 0:TOP, :] = jnp.zeros((4, NB, TOP, 128), jnp.float32)

    @pl.when(gy == last_gy)
    def _():
        for _, vmem in arrays:
            vmem[:, :, TOP + ROWS :, :] = jnp.zeros((4, NB, TOP, 128), jnp.float32)

    edges = jnp.where(gy > 0, 1, 0) + jnp.where(gy < last_gy, 1, 0)
    pl.semaphore_wait(barrier, 5 + edges)

    def remote(src, dst, send, recv, who):
        return pltpu.make_async_remote_copy(
            src_ref=src, dst_ref=dst, send_sem=send, recv_sem=recv,
            device_id=here[who], device_id_type=MESH,
        )

    def edge_copies(down):
        for at, (hbm, vmem) in enumerate(arrays):
            for k in range(NB):
                i = at * NB + k
                taken = ROWS - MARGIN if down else 0
                put = TOP - MARGIN if down else TOP + ROWS
                yield remote(
                    hbm.at[:, taken : taken + MARGIN, 128 * k : 128 * (k + 1)],
                    vmem.at[:, k, put : put + MARGIN, :],
                    edge_s.at[down, i], edge_r.at[down, i], "down" if down else "up",
                )

    @pl.when(gy > 0)
    def _():
        for copy in edge_copies(0):
            copy.start()

    @pl.when(gy < last_gy)
    def _():
        for copy in edge_copies(1):
            copy.start()

    def take_edges():
        @pl.when(gy > 0)
        def _():
            for copy in edge_copies(1):
                copy.wait_recv()

        @pl.when(gy < last_gy)
        def _():
            for copy in edge_copies(0):
                copy.wait_recv()

    pieces = (
        (0, TOP, ROWS),
        (0, TOP - MARGIN, MARGIN),
        (0, TOP + ROWS, MARGIN),
        (1, TOP - 2, ROWS + 4),
        (2, TOP - 1, ROWS + 2),
        (3, TOP, ROWS),
    )

    def near_copy(j, ref, stride):
        n, row, rows = pieces[j]
        return remote(
            ref.at[(1 - core) * stride, :, row : row + rows, :],
            got.at[core, n, :, row : row + rows, :], near_s.at[j], near_r.at[j], "partner",
        )

    def far_copy(j, ref, stride, way):
        n, row, rows = pieces[j]
        return remote(
            ref.at[core * stride, 2 * way : 2 * way + 2, row : row + rows, :],
            relay.at[n, way, :, row : row + rows, :], far_s.at[j, way], hop_r.at[j, way],
            "minus" if way else "plus",
        )

    def hop_copy(j, way):
        n, row, rows = pieces[j]
        return remote(
            relay.at[n, way, :, row : row + rows, :],
            got.at[1 - core, n, 2 * way : 2 * way + 2, row : row + rows, :],
            hop_s.at[j, way], far_r.at[j, way],
            "target_of_plus" if way else "target_of_minus",
        )

    sends = []

    def go(copy):
        copy.start()
        sends.append(copy)

    def send_faces(j, ref, stride):
        for way in range(2):
            go(far_copy(j, ref, stride, way))
        go(near_copy(j, ref, stride))

    def relay_on(j):
        for way in range(2):
            far_copy(j, u0, 3, way).wait_recv()
            go(hop_copy(j, way))

    def wait_faces(j):
        near_copy(j, u0, 3).wait_recv()
        for way in range(2):
            hop_copy(j, way).wait_recv()

    lane = lax.broadcasted_iota(jnp.int32, (NB, 8, 128), 2)
    at_first, at_last = lane == 0, lane == 127
    zero = jnp.zeros((1, 8, 128), jnp.float32)

    def step(planes, which, dest, tiles, first, data=None, fresh=False, drop=0):
        def tile(row):
            here_rows = pl.ds(row, 8)

            def read(p, shift=0):
                ref, i = planes[p]
                return ref[i, :, pl.ds(row + shift, 8), :]

            need = sorted({q for p in which for q in (p - 1, p, p + 1) if 0 <= q < 4})
            cells = {p: read(p) for p in need}

            def ghost(side, face):
                if data is None:
                    return face * FACE_W
                return face * FACE_W + got[side, data, :, here_rows, :] * DATA_W

            results = []
            for p in which:
                c = cells[p]
                minus_x = cells[p - 1] if p > 0 else ghost(0, c)
                plus_x = cells[p + 1] if p < 3 else ghost(1, c)
                ahead, behind = pltpu.roll(c, 127, 2), pltpu.roll(c, 1, 2)
                plus_z = jnp.where(at_last, jnp.concatenate([ahead[1:], zero], 0), ahead)
                minus_z = jnp.where(at_first, jnp.concatenate([zero, behind[:-1]], 0), behind)
                total = (plus_x + minus_x) + (read(p, 1) + read(p, -1)) + (plus_z + minus_z)
                k = kb[p, :, here_rows, :]
                v = vb[p, :, here_rows, :]
                q = rb[p, :, here_rows, :]
                a = (1.0 - 6.0 * k) - (v + q) if fresh else ab[p, :, here_rows, :]
                inner = a + q * pl.reciprocal(1.0 + c * c)
                results.append((p, a, c * inner + (k * total + v * minus_x)))
            return results

        def store(row, results):
            for p, a, value in results:
                if fresh:
                    ab[p, :, pl.ds(row, 8), :] = a
                ref, i = dest[p]
                ref[i, :, pl.ds(row - drop, 8), :] = value

        begin, end = tiles
        pairs = (end - begin) // 2

        def body(t, carry):
            row = pl.multiple_of(t * 16, 16) + (first + 8 * begin)
            one, two = tile(row), tile(row + 8)
            store(row, one)
            store(row + 8, two)
            return carry

        if pairs > 1:
            lax.fori_loop(0, pairs, body, 0)
        elif pairs:
            body(0, 0)
        if (end - begin) % 2:
            row = first + 8 * (end - 1)
            store(row, tile(row))

    def whole(ref):
        return [(ref, p) for p in range(4)]

    a0, a1, a2 = whole(u0), whole(u1), whole(u2)
    a3 = {0: (u3, 0), 3: (u3, 1)}
    b1 = [(v1, 0), (u1, 1), (u1, 2), (v1, 1)]
    b2, b3, b4 = whole(v2), whole(v3), whole(o4)
    outer, inner = (0, 3), (1, 2)
    wide = ((0, 17), TOP - MARGIN)
    plain = ((0, 16), TOP)

    for copy in loads[:NB]:
        copy.wait()
    send_faces(0, u0, 3)
    for copy in loads[NB:]:
        copy.wait()
    for which in (outer, inner):
        step(a0, which, a1, (1, 15), TOP - MARGIN, fresh=True)
    take_edges()
    send_faces(1, u0, 3)
    send_faces(2, u0, 3)
    for tiles in ((0, 1), (15, 17)):
        step(a0, outer, a1, tiles, TOP - MARGIN, fresh=True)
    send_faces(3, u1, 3)
    for tiles in ((0, 1), (15, 17)):
        step(a0, inner, a1, tiles, TOP - MARGIN, fresh=True)
    relay_on(0)
    step(a1, outer, a2, *wide)
    send_faces(4, u2, 3)
    step(a1, inner, a2, *wide)
    step(a2, outer, a3, *plain)
    send_faces(5, u3, 1)
    for j in (1, 2, 3):
        relay_on(j)
    for j in (0, 1, 2):
        wait_faces(j)
    step(a0, outer, {0: b1[0], 3: b1[3]}, *wide, data=0)
    relay_on(4)
    step(b1, inner, b2, *wide)
    relay_on(5)
    wait_faces(3)
    step(b1, outer, b2, *wide, data=1)
    step(b2, inner, b3, *wide)
    wait_faces(4)
    step(b2, outer, b3, *wide, data=2)
    step(b3, inner, b4, *plain, drop=TOP)

    def put(first, count, at):
        copies = []
        for k in range(NB):
            copy = pltpu.make_async_copy(
                o4.at[first : first + count, k],
                out.at[first : first + count, :, 128 * k : 128 * (k + 1)],
                out_sem.at[at * NB + k],
            )
            copy.start()
            copies.append(copy)
        return copies

    puts = put(1, 2, 0)
    wait_faces(5)
    step(b3, outer, b4, *plain, data=3, drop=TOP)
    puts += put(0, 1, 1) + put(3, 1, 2)
    for copy in sends:
        copy.wait_send()

    @pl.when(gy > 0)
    def _():
        for copy in edge_copies(0):
            copy.wait_send()

    @pl.when(gy < last_gy)
    def _():
        for copy in edge_copies(1):
            copy.wait_send()

    for copy in puts:
        copy.wait()


def local(initial, kappa, velocity, rate):
    tall = ROWS + 2 * TOP
    f32 = lambda *shape: pltpu.VMEM(shape, jnp.float32)
    full, pair = f32(4, NB, tall, 128), f32(2, NB, tall, 128)
    dma = pltpu.SemaphoreType.DMA
    return pl.pallas_call(
        kernel,
        out_shape=jax.ShapeDtypeStruct(initial.shape, jnp.float32),
        in_specs=[pl.BlockSpec(memory_space=pl.ANY)] * 4,
        out_specs=pl.BlockSpec(memory_space=pl.ANY),
        scratch_shapes=[
            full, full, full, pair, pair, full, full, f32(4, NB, ROWS, 128),
            full, full, full, full,
            f32(2, STEPS, NB, tall, 128), f32(STEPS, 2, 2, tall, 128),
            dma((16,)), dma((12,)), dma((6,)), dma((6,)),
            dma((6, 2)), dma((6, 2)), dma((6, 2)), dma((6, 2)),
            dma((2, 16)), dma((2, 16)),
        ],
        compiler_params=pltpu.CompilerParams(collective_id=0, has_side_effects=True),
        name="window",
    )(initial, kappa, velocity, rate)


def solution(mesh):
    placed = P("gx", "gy", None)
    return jax.shard_map(
        local, mesh=mesh, in_specs=(placed,) * 4, out_specs=placed, check_vma=False
    )
```

```python
import jax
import jax.numpy as jnp
from jax import lax
from jax.experimental import pallas as pl
from jax.experimental.pallas import tpu as pltpu
from jax.sharding import PartitionSpec as P

STEPS = 4
robin_p = 0.6
MESH = pl.DeviceIdType.MESH
FACE_W = (1.0 - robin_p / 2) / (1.0 + robin_p / 2)
SENT_W = (1.0 - FACE_W) + robin_p * (1.0 + FACE_W) / 2
DATA_W = SENT_W / (1.0 + robin_p / 2)
NB = 4
ROWS = 128
TOP = 8
MARGIN = 4


def places():
    gx, gy = lax.axis_index("gx"), lax.axis_index("gy")
    ngx = lax.axis_size("gx")
    core = gx % 2
    x = ((gx // 2) % 2) * 2 + gy // 4

    def chip(step):
        other = (x + step + 4) % 4
        return ((gx // 4) * 4 + (other // 2) * 2 + core, (other % 2) * 4 + gy % 4)

    def target(of):
        return ((of[0] + 2 * core - 1 + ngx) % ngx, of[1])

    source_gx = (gx - 1 + 2 * core + ngx) % ngx
    source_x = ((source_gx // 2) % 2) * 2 + gy // 4

    def source_relay(step):
        other = (source_x + step + 4) % 4
        return (
            (source_gx // 4) * 4 + (other // 2) * 2 + source_gx % 2,
            (other % 2) * 4 + gy % 4,
        )

    plus, minus = chip(1), chip(-1)
    return dict(
        core=core,
        gy=gy,
        partner=(gx + 1 - 2 * core, gy),
        plus=plus,
        minus=minus,
        target_of_minus=target(minus),
        target_of_plus=target(plus),
        deliver_a=source_relay(1),
        deliver_b=source_relay(-1),
        up=(gx, gy - 1),
        down=(gx, gy + 1),
    )


def kernel(
    init, kap, vel, rat, out,
    u0, u1, u2, u3, v1, v2, v3, kb, vb, rb, ab, got, relay,
    load_sem, near_s, near_r, far_s, far_r, hop_s, hop_r, edge_s, edge_r,
):
    here = places()
    core, gy = here["core"], here["gy"]
    last_gy = lax.axis_size("gy") - 1
    arrays = ((init, u0), (kap, kb), (vel, vb), (rat, rb))

    loads = []
    for at, (hbm, vmem) in enumerate(arrays):
        for k in range(NB):
            copy = pltpu.make_async_copy(
                hbm.at[:, :, 128 * k : 128 * (k + 1)],
                vmem.at[:, k, TOP : TOP + ROWS, :],
                load_sem.at[at * NB + k],
            )
            copy.start()
            loads.append(copy)

    barrier = pltpu.get_barrier_semaphore()
    for who in ("partner", "plus", "minus", "deliver_a", "deliver_b"):
        pl.semaphore_signal(barrier, inc=1, device_id=here[who], device_id_type=MESH)

    @pl.when(gy > 0)
    def _():
        pl.semaphore_signal(barrier, inc=1, device_id=here["up"], device_id_type=MESH)

    @pl.when(gy < last_gy)
    def _():
        pl.semaphore_signal(barrier, inc=1, device_id=here["down"], device_id_type=MESH)

    @pl.when(gy == 0)
    def _():
        for _, vmem in arrays:
            vmem[:, :, 0:TOP, :] = jnp.zeros((4, NB, TOP, 128), jnp.float32)

    @pl.when(gy == last_gy)
    def _():
        for _, vmem in arrays:
            vmem[:, :, TOP + ROWS :, :] = jnp.zeros((4, NB, TOP, 128), jnp.float32)

    edges = jnp.where(gy > 0, 1, 0) + jnp.where(gy < last_gy, 1, 0)
    pl.semaphore_wait(barrier, 5 + edges)

    def remote(src, dst, send, recv, who):
        return pltpu.make_async_remote_copy(
            src_ref=src, dst_ref=dst, send_sem=send, recv_sem=recv,
            device_id=here[who], device_id_type=MESH,
        )

    pieces = (
        (0, TOP, ROWS, 0, 1),
        (0, TOP, ROWS, 1, 1),
        (0, TOP - MARGIN, MARGIN, 0, 2),
        (0, TOP + ROWS, MARGIN, 0, 2),
        (1, TOP - 2, ROWS + 4, 0, 2),
        (2, TOP - 1, ROWS + 2, 0, 2),
        (3, TOP, ROWS, 0, 1),
        (3, TOP, ROWS, 1, 1),
    )

    def near_copy(n, ref, stride):
        row = (TOP - MARGIN, TOP - 2, TOP - 1, TOP)[n]
        rows = ROWS + 2 * (TOP - row)
        return remote(
            ref.at[(1 - core) * stride, :, row : row + rows, :],
            got.at[core, n, :, row : row + rows, :], near_s.at[n], near_r.at[n], "partner",
        )

    def far_copy(j, ref, stride, way):
        n, row, rows, k, blocks = pieces[j]
        if ref is init:
            lanes = slice(128 * (2 * way + k), 128 * (2 * way + k + 1))
            src, dst = ref.at[core * stride, :, lanes], relay.at[n, way, k, row : row + rows, :]
        else:
            src = ref.at[core * stride, 2 * way + k : 2 * way + k + blocks, row : row + rows, :]
            dst = relay.at[n, way, k : k + blocks, row : row + rows, :]
        return remote(
            src, dst, far_s.at[j, way], hop_r.at[j, way], "minus" if way else "plus"
        )

    def hop_copy(j, way):
        n, row, rows, k, blocks = pieces[j]
        return remote(
            relay.at[n, way, k : k + blocks, row : row + rows, :],
            got.at[1 - core, n, 2 * way + k : 2 * way + k + blocks, row : row + rows, :],
            hop_s.at[j, way], far_r.at[j, way],
            "target_of_plus" if way else "target_of_minus",
        )

    sends = []

    def go(copy):
        copy.start()
        sends.append(copy)

    def send_far(js, ref, stride):
        for j in js:
            for way in range(2):
                go(far_copy(j, ref, stride, way))

    def relay_on(js):
        for j in js:
            for way in range(2):
                far_copy(j, u0, 3, way).wait_recv()
                go(hop_copy(j, way))

    def wait_faces(n):
        near_copy(n, u0, 3).wait_recv()
        for j in range(len(pieces)):
            if pieces[j][0] == n:
                for way in range(2):
                    hop_copy(j, way).wait_recv()

    send_far((0, 1), init, 3)

    def edge_copies(down):
        for i, (_, vmem) in enumerate(arrays):
            rows = MARGIN if i == 0 else MARGIN - 1
            taken = TOP + ROWS - rows if down else TOP
            put = TOP - rows if down else TOP + ROWS
            yield remote(
                vmem.at[:, :, taken : taken + rows, :], vmem.at[:, :, put : put + rows, :],
                edge_s.at[down, i], edge_r.at[down, i], "down" if down else "up",
            )

    for copy in loads:
        copy.wait()

    @pl.when(gy > 0)
    def _():
        for copy in edge_copies(0):
            copy.start()

    @pl.when(gy < last_gy)
    def _():
        for copy in edge_copies(1):
            copy.start()

    def take_edges():
        @pl.when(gy > 0)
        def _():
            for copy in edge_copies(1):
                copy.wait_recv()

        @pl.when(gy < last_gy)
        def _():
            for copy in edge_copies(0):
                copy.wait_recv()

    lane = lax.broadcasted_iota(jnp.int32, (NB, 8, 128), 2)
    at_first, at_last = lane == 0, lane == 127
    zero = jnp.zeros((1, 8, 128), jnp.float32)

    def step(planes, which, dest, tiles, first, data=None, fresh=False):
        def tile(row):
            here_rows = pl.ds(row, 8)

            def read(p, shift=0):
                ref, i = planes[p]
                return ref[i, :, pl.ds(row + shift, 8), :]

            need = sorted({q for p in which for q in (p - 1, p, p + 1) if 0 <= q < 4})
            cells = {p: read(p) for p in need}

            def ghost(side, face):
                if data is None:
                    return face * FACE_W
                return face * FACE_W + got[side, data, :, here_rows, :] * DATA_W

            results = []
            for p in which:
                c = cells[p]
                minus_x = cells[p - 1] if p > 0 else ghost(0, c)
                plus_x = cells[p + 1] if p < 3 else ghost(1, c)
                ahead, behind = pltpu.roll(c, 127, 2), pltpu.roll(c, 1, 2)
                plus_z = jnp.where(at_last, jnp.concatenate([ahead[1:], zero], 0), ahead)
                minus_z = jnp.where(at_first, jnp.concatenate([zero, behind[:-1]], 0), behind)
                total = (plus_x + minus_x) + (read(p, 1) + read(p, -1)) + (plus_z + minus_z)
                k = kb[p, :, here_rows, :]
                v = vb[p, :, here_rows, :]
                q = rb[p, :, here_rows, :]
                a = (1.0 - 6.0 * k) - (v + q) if fresh else ab[p, :, here_rows, :]
                inner = a + q * pl.reciprocal(1.0 + c * c)
                results.append((p, a, c * inner + (k * total + v * minus_x)))
            return results

        def store(row, results):
            for p, a, value in results:
                if fresh:
                    ab[p, :, pl.ds(row, 8), :] = a
                if dest is None:
                    for k in range(NB):
                        out[p, pl.ds(row - TOP, 8), 128 * k : 128 * (k + 1)] = value[k]
                else:
                    ref, i = dest[p]
                    ref[i, :, pl.ds(row, 8), :] = value

        begin, end = tiles
        pairs = (end - begin) // 2

        def body(t, carry):
            row = pl.multiple_of(t * 16, 16) + (first + 8 * begin)
            one, two = tile(row), tile(row + 8)
            store(row, one)
            store(row + 8, two)
            return carry

        if pairs > 1:
            lax.fori_loop(0, pairs, body, 0)
        elif pairs:
            body(0, 0)
        if (end - begin) % 2:
            row = first + 8 * (end - 1)
            store(row, tile(row))

    def whole(ref):
        return [(ref, p) for p in range(4)]

    a0, a1, a2 = whole(u0), whole(u1), whole(u2)
    a3 = {0: (u3, 0), 3: (u3, 1)}
    b1 = [(v1, 0), (u1, 1), (u1, 2), (v1, 1)]
    b2, b3 = whole(v2), whole(v3)
    outer, inner = (0, 3), (1, 2)
    wide = ((0, 17), TOP - MARGIN)
    plain = ((0, 16), TOP)

    for which in (outer, inner):
        step(a0, which, a1, (1, 15), TOP - MARGIN, fresh=True)
    relay_on((0, 1))
    take_edges()
    for tiles in ((0, 1), (15, 17)):
        step(a0, outer, a1, tiles, TOP - MARGIN, fresh=True)
    send_far((4,), u1, 3)
    send_far((2, 3), u0, 3)
    go(near_copy(0, u0, 3))
    go(near_copy(1, u1, 3))
    for tiles in ((0, 1), (15, 17)):
        step(a0, inner, a1, tiles, TOP - MARGIN, fresh=True)
    step(a1, outer, a2, *wide)
    send_far((5,), u2, 3)
    go(near_copy(2, u2, 3))
    step(a1, inner, a2, *wide)
    step(a2, outer, a3, *plain)
    send_far((6, 7), u3, 1)
    go(near_copy(3, u3, 1))
    relay_on((4, 2, 3))
    wait_faces(0)
    step(a0, outer, {0: b1[0], 3: b1[3]}, *wide, data=0)
    relay_on((5,))
    step(b1, inner, b2, *wide)
    relay_on((6, 7))
    wait_faces(1)
    step(b1, outer, b2, *wide, data=1)
    step(b2, inner, b3, *wide)
    wait_faces(2)
    step(b2, outer, b3, *wide, data=2)
    step(b3, inner, None, *plain)
    wait_faces(3)
    step(b3, outer, None, *plain, data=3)
    for copy in sends:
        copy.wait_send()

    @pl.when(gy > 0)
    def _():
        for copy in edge_copies(0):
            copy.wait_send()

    @pl.when(gy < last_gy)
    def _():
        for copy in edge_copies(1):
            copy.wait_send()


def local(initial, kappa, velocity, rate):
    tall = ROWS + 2 * TOP
    f32 = lambda *shape: pltpu.VMEM(shape, jnp.float32)
    full, pair = f32(4, NB, tall, 128), f32(2, NB, tall, 128)
    dma = pltpu.SemaphoreType.DMA
    return pl.pallas_call(
        kernel,
        out_shape=jax.ShapeDtypeStruct(initial.shape, jnp.float32),
        in_specs=[pl.BlockSpec(memory_space=pltpu.HBM)] * 4,
        out_specs=pl.BlockSpec(memory_space=pltpu.VMEM),
        scratch_shapes=[
            full, full, full, pair, pair, full, full,
            full, full, full, full,
            f32(2, STEPS, NB, tall, 128), f32(STEPS, 2, 2, tall, 128),
            dma((16,)), dma((STEPS,)), dma((STEPS,)),
            dma((8, 2)), dma((8, 2)), dma((8, 2)), dma((8, 2)),
            dma((2, 4)), dma((2, 4)),
        ],
        compiler_params=pltpu.CompilerParams(
            collective_id=0, has_side_effects=True, vmem_limit_bytes=40 * 2**20
        ),
        name="window",
    )(*(pltpu.with_memory_space_constraint(x, pltpu.HBM) for x in (initial, kappa, velocity, rate)))


def solution(mesh):
    placed = P("gx", "gy", None)
    return jax.shard_map(
        local, mesh=mesh, in_specs=(placed,) * 4, out_specs=placed, check_vma=False
    )
```

```python
import jax
import jax.numpy as jnp
from jax import lax
from jax.experimental import pallas as pl
from jax.experimental.pallas import tpu as pltpu
from jax.sharding import PartitionSpec as P

STEPS = 4
robin_p = 0.6
MESH = pl.DeviceIdType.MESH
FACE_W = (1.0 - robin_p / 2) / (1.0 + robin_p / 2)
SENT_W = (1.0 - FACE_W) + robin_p * (1.0 + FACE_W) / 2
DATA_W = SENT_W / (1.0 + robin_p / 2)
NB = 4
ROWS = 128
TOP = 8
MARGIN = 4


def places():
    gx, gy = lax.axis_index("gx"), lax.axis_index("gy")
    ngx = lax.axis_size("gx")
    core = gx % 2
    x = ((gx // 2) % 2) * 2 + gy // 4

    def chip(step):
        other = (x + step + 4) % 4
        return ((gx // 4) * 4 + (other // 2) * 2 + core, (other % 2) * 4 + gy % 4)

    def target(of):
        return ((of[0] + 2 * core - 1 + ngx) % ngx, of[1])

    source_gx = (gx - 1 + 2 * core + ngx) % ngx
    source_x = ((source_gx // 2) % 2) * 2 + gy // 4

    def source_relay(step):
        other = (source_x + step + 4) % 4
        return (
            (source_gx // 4) * 4 + (other // 2) * 2 + source_gx % 2,
            (other % 2) * 4 + gy % 4,
        )

    plus, minus = chip(1), chip(-1)
    return dict(
        core=core,
        gy=gy,
        partner=(gx + 1 - 2 * core, gy),
        plus=plus,
        minus=minus,
        target_of_minus=target(minus),
        target_of_plus=target(plus),
        deliver_a=source_relay(1),
        deliver_b=source_relay(-1),
        up=(gx, gy - 1),
        down=(gx, gy + 1),
    )


def kernel(
    init, kap, vel, rat, out,
    u0, u1, u2, u3, v1, v2, v3, kb, vb, rb, ab, got, relay,
    load_sem, near_s, near_r, far_s, far_r, hop_s, hop_r, edge_s, edge_r,
):
    here = places()
    core, gy = here["core"], here["gy"]
    last_gy = lax.axis_size("gy") - 1
    arrays = ((init, u0), (kap, kb), (vel, vb), (rat, rb))

    loads = []
    for at, (hbm, vmem) in enumerate(arrays):
        for k in range(NB):
            copy = pltpu.make_async_copy(
                hbm.at[:, :, 128 * k : 128 * (k + 1)],
                vmem.at[:, k, TOP : TOP + ROWS, :],
                load_sem.at[at * NB + k],
            )
            copy.start()
            loads.append(copy)

    barrier = pltpu.get_barrier_semaphore()
    for who in ("partner", "plus", "minus", "deliver_a", "deliver_b"):
        pl.semaphore_signal(barrier, inc=1, device_id=here[who], device_id_type=MESH)

    @pl.when(gy > 0)
    def _():
        pl.semaphore_signal(barrier, inc=1, device_id=here["up"], device_id_type=MESH)

    @pl.when(gy < last_gy)
    def _():
        pl.semaphore_signal(barrier, inc=1, device_id=here["down"], device_id_type=MESH)

    @pl.when(gy == 0)
    def _():
        for _, vmem in arrays:
            vmem[:, :, 0:TOP, :] = jnp.zeros((4, NB, TOP, 128), jnp.float32)

    @pl.when(gy == last_gy)
    def _():
        for _, vmem in arrays:
            vmem[:, :, TOP + ROWS :, :] = jnp.zeros((4, NB, TOP, 128), jnp.float32)

    edges = jnp.where(gy > 0, 1, 0) + jnp.where(gy < last_gy, 1, 0)
    pl.semaphore_wait(barrier, 5 + edges)

    def remote(src, dst, send, recv, who):
        return pltpu.make_async_remote_copy(
            src_ref=src, dst_ref=dst, send_sem=send, recv_sem=recv,
            device_id=here[who], device_id_type=MESH,
        )

    pieces = (
        (0, TOP, ROWS, 0, 1),
        (0, TOP, ROWS, 1, 1),
        (0, TOP - MARGIN, MARGIN, 0, 2),
        (0, TOP + ROWS, MARGIN, 0, 2),
        (1, TOP - 2, ROWS + 4, 0, 2),
        (2, TOP - 1, ROWS + 2, 0, 2),
        (3, TOP, ROWS, 0, 1),
        (3, TOP, ROWS, 1, 1),
    )

    def near_copy(n, ref, stride):
        row = (TOP - MARGIN, TOP - 2, TOP - 1, TOP)[n]
        rows = ROWS + 2 * (TOP - row)
        return remote(
            ref.at[(1 - core) * stride, :, row : row + rows, :],
            got.at[core, n, :, row : row + rows, :], near_s.at[n], near_r.at[n], "partner",
        )

    def far_copy(j, ref, stride, way):
        n, row, rows, k, blocks = pieces[j]
        if ref is init:
            lanes = slice(128 * (2 * way + k), 128 * (2 * way + k + 1))
            src, dst = ref.at[core * stride, :, lanes], relay.at[n, way, k, row : row + rows, :]
        else:
            src = ref.at[core * stride, 2 * way + k : 2 * way + k + blocks, row : row + rows, :]
            dst = relay.at[n, way, k : k + blocks, row : row + rows, :]
        return remote(
            src, dst, far_s.at[j, way], hop_r.at[j, way], "minus" if way else "plus"
        )

    def hop_copy(j, way):
        n, row, rows, k, blocks = pieces[j]
        return remote(
            relay.at[n, way, k : k + blocks, row : row + rows, :],
            got.at[1 - core, n, 2 * way + k : 2 * way + k + blocks, row : row + rows, :],
            hop_s.at[j, way], far_r.at[j, way],
            "target_of_plus" if way else "target_of_minus",
        )

    sends = []

    def go(copy):
        copy.start()
        sends.append(copy)

    def send_far(js, ref, stride):
        for j in js:
            for way in range(2):
                go(far_copy(j, ref, stride, way))

    def relay_on(js):
        for j in js:
            for way in range(2):
                far_copy(j, u0, 3, way).wait_recv()
                go(hop_copy(j, way))

    def wait_faces(n):
        near_copy(n, u0, 3).wait_recv()
        for j in range(len(pieces)):
            if pieces[j][0] == n:
                for way in range(2):
                    hop_copy(j, way).wait_recv()

    def edge_copies(down):
        for i, (_, vmem) in enumerate(arrays):
            rows = MARGIN if i == 0 else MARGIN - 1
            taken = TOP + ROWS - rows if down else TOP
            put = TOP - rows if down else TOP + ROWS
            yield remote(
                vmem.at[:, :, taken : taken + rows, :], vmem.at[:, :, put : put + rows, :],
                edge_s.at[down, i], edge_r.at[down, i], "down" if down else "up",
            )

    for copy in loads:
        copy.wait()

    @pl.when(gy > 0)
    def _():
        for copy in edge_copies(0):
            copy.start()

    @pl.when(gy < last_gy)
    def _():
        for copy in edge_copies(1):
            copy.start()

    def take_edges():
        @pl.when(gy > 0)
        def _():
            for copy in edge_copies(1):
                copy.wait_recv()

        @pl.when(gy < last_gy)
        def _():
            for copy in edge_copies(0):
                copy.wait_recv()

    send_far((0, 1), u0, 3)

    lane = lax.broadcasted_iota(jnp.int32, (NB, 8, 128), 2)
    at_first, at_last = lane == 0, lane == 127
    zero = jnp.zeros((1, 8, 128), jnp.float32)

    def step(planes, which, dest, tiles, first, data=None, fresh=False):
        def tile(row):
            here_rows = pl.ds(row, 8)

            def read(p, shift=0):
                ref, i = planes[p]
                return ref[i, :, pl.ds(row + shift, 8), :]

            need = sorted({q for p in which for q in (p - 1, p, p + 1) if 0 <= q < 4})
            cells = {p: read(p) for p in need}

            def ghost(side, face):
                if data is None:
                    return face * FACE_W
                return face * FACE_W + got[side, data, :, here_rows, :] * DATA_W

            results = []
            for p in which:
                c = cells[p]
                minus_x = cells[p - 1] if p > 0 else ghost(0, c)
                plus_x = cells[p + 1] if p < 3 else ghost(1, c)
                ahead, behind = pltpu.roll(c, 127, 2), pltpu.roll(c, 1, 2)
                plus_z = jnp.where(at_last, jnp.concatenate([ahead[1:], zero], 0), ahead)
                minus_z = jnp.where(at_first, jnp.concatenate([zero, behind[:-1]], 0), behind)
                total = (plus_x + minus_x) + (read(p, 1) + read(p, -1)) + (plus_z + minus_z)
                k = kb[p, :, here_rows, :]
                v = vb[p, :, here_rows, :]
                q = rb[p, :, here_rows, :]
                a = (1.0 - 6.0 * k) - (v + q) if fresh else ab[p, :, here_rows, :]
                inner = a + q * pl.reciprocal(1.0 + c * c)
                results.append((p, a, c * inner + (k * total + v * minus_x)))
            return results

        def store(row, results):
            for p, a, value in results:
                if fresh:
                    ab[p, :, pl.ds(row, 8), :] = a
                if dest is None:
                    for k in range(NB):
                        out[p, pl.ds(row - TOP, 8), 128 * k : 128 * (k + 1)] = value[k]
                else:
                    ref, i = dest[p]
                    ref[i, :, pl.ds(row, 8), :] = value

        begin, end = tiles
        pairs = (end - begin) // 2

        def body(t, carry):
            row = pl.multiple_of(t * 16, 16) + (first + 8 * begin)
            one, two = tile(row), tile(row + 8)
            store(row, one)
            store(row + 8, two)
            return carry

        if pairs > 1:
            lax.fori_loop(0, pairs, body, 0)
        elif pairs:
            body(0, 0)
        if (end - begin) % 2:
            row = first + 8 * (end - 1)
            store(row, tile(row))

    def whole(ref):
        return [(ref, p) for p in range(4)]

    a0, a1, a2 = whole(u0), whole(u1), whole(u2)
    a3 = {0: (u3, 0), 3: (u3, 1)}
    b1 = [(v1, 0), (u1, 1), (u1, 2), (v1, 1)]
    b2, b3 = whole(v2), whole(v3)
    outer, inner = (0, 3), (1, 2)
    wide = ((0, 17), TOP - MARGIN)
    plain = ((0, 16), TOP)

    for which in (outer, inner):
        step(a0, which, a1, (1, 15), TOP - MARGIN, fresh=True)
    relay_on((0, 1))
    take_edges()
    for tiles in ((0, 1), (15, 17)):
        step(a0, outer, a1, tiles, TOP - MARGIN, fresh=True)
    send_far((4,), u1, 3)
    send_far((2, 3), u0, 3)
    go(near_copy(0, u0, 3))
    go(near_copy(1, u1, 3))
    for tiles in ((0, 1), (15, 17)):
        step(a0, inner, a1, tiles, TOP - MARGIN, fresh=True)
    step(a1, outer, a2, *wide)
    send_far((5,), u2, 3)
    go(near_copy(2, u2, 3))
    step(a1, inner, a2, *wide)
    step(a2, outer, a3, *plain)
    relay_on((4, 2, 3))
    send_far((6, 7), u3, 1)
    go(near_copy(3, u3, 1))
    wait_faces(0)
    step(a0, outer, {0: b1[0], 3: b1[3]}, *wide, data=0)
    relay_on((5,))
    step(b1, inner, b2, *wide)
    relay_on((6, 7))
    wait_faces(1)
    step(b1, outer, b2, *wide, data=1)
    step(b2, inner, b3, *wide)
    wait_faces(2)
    step(b2, outer, b3, *wide, data=2)
    step(b3, inner, None, *plain)
    wait_faces(3)
    step(b3, outer, None, *plain, data=3)
    for copy in sends:
        copy.wait_send()

    @pl.when(gy > 0)
    def _():
        for copy in edge_copies(0):
            copy.wait_send()

    @pl.when(gy < last_gy)
    def _():
        for copy in edge_copies(1):
            copy.wait_send()


def local(initial, kappa, velocity, rate):
    tall = ROWS + 2 * TOP
    f32 = lambda *shape: pltpu.VMEM(shape, jnp.float32)
    full, pair = f32(4, NB, tall, 128), f32(2, NB, tall, 128)
    dma = pltpu.SemaphoreType.DMA
    return pl.pallas_call(
        kernel,
        out_shape=jax.ShapeDtypeStruct(initial.shape, jnp.float32),
        in_specs=[pl.BlockSpec(memory_space=pltpu.HBM)] * 4,
        out_specs=pl.BlockSpec(memory_space=pltpu.VMEM),
        scratch_shapes=[
            full, full, full, pair, pair, full, full,
            full, full, full, full,
            f32(2, STEPS, NB, tall, 128), f32(STEPS, 2, 2, tall, 128),
            dma((16,)), dma((STEPS,)), dma((STEPS,)),
            dma((8, 2)), dma((8, 2)), dma((8, 2)), dma((8, 2)),
            dma((2, 4)), dma((2, 4)),
        ],
        compiler_params=pltpu.CompilerParams(
            collective_id=0, has_side_effects=True, vmem_limit_bytes=40 * 2**20
        ),
        name="window",
    )(*(pltpu.with_memory_space_constraint(x, pltpu.HBM) for x in (initial, kappa, velocity, rate)))


def solution(mesh):
    placed = P("gx", "gy", None)
    return jax.shard_map(
        local, mesh=mesh, in_specs=(placed,) * 4, out_specs=placed, check_vma=False
    )
```

```python
import jax
import jax.numpy as jnp
from jax import lax
from jax.experimental import pallas as pl
from jax.experimental.pallas import tpu as pltpu
from jax.sharding import PartitionSpec as P

STEPS = 4
robin_p = 0.6
MESH = pl.DeviceIdType.MESH
FACE_W = (1.0 - robin_p / 2) / (1.0 + robin_p / 2)
SENT_W = (1.0 - FACE_W) + robin_p * (1.0 + FACE_W) / 2
DATA_W = SENT_W / (1.0 + robin_p / 2)
NB = 4
ROWS = 128
TOP = 8
MARGIN = 4


def places():
    gx, gy = lax.axis_index("gx"), lax.axis_index("gy")
    ngx = lax.axis_size("gx")
    core = gx % 2
    x = ((gx // 2) % 2) * 2 + gy // 4

    def chip(step):
        other = (x + step + 4) % 4
        return ((gx // 4) * 4 + (other // 2) * 2 + core, (other % 2) * 4 + gy % 4)

    def target(of):
        return ((of[0] + 2 * core - 1 + ngx) % ngx, of[1])

    source_gx = (gx - 1 + 2 * core + ngx) % ngx
    source_x = ((source_gx // 2) % 2) * 2 + gy // 4

    def source_relay(step):
        other = (source_x + step + 4) % 4
        return (
            (source_gx // 4) * 4 + (other // 2) * 2 + source_gx % 2,
            (other % 2) * 4 + gy % 4,
        )

    plus, minus = chip(1), chip(-1)
    return dict(
        core=core,
        gy=gy,
        partner=(gx + 1 - 2 * core, gy),
        plus=plus,
        minus=minus,
        target_of_minus=target(minus),
        target_of_plus=target(plus),
        deliver_a=source_relay(1),
        deliver_b=source_relay(-1),
        up=(gx, gy - 1),
        down=(gx, gy + 1),
    )


def kernel(
    init, kap, vel, rat, out,
    u0, u1, u2, u3, v1, v2, v3, kb, vb, rb, ab, got, relay,
    load_sem, near_s, near_r, far_s, far_r, hop_s, hop_r, edge_s, edge_r,
):
    here = places()
    core, gy = here["core"], here["gy"]
    last_gy = lax.axis_size("gy") - 1
    arrays = ((init, u0), (kap, kb), (vel, vb), (rat, rb))

    loads = []
    for at, (hbm, vmem) in enumerate(arrays):
        for k in range(NB):
            copy = pltpu.make_async_copy(
                hbm.at[:, :, 128 * k : 128 * (k + 1)],
                vmem.at[:, k, TOP : TOP + ROWS, :],
                load_sem.at[at * NB + k],
            )
            copy.start()
            loads.append(copy)

    barrier = pltpu.get_barrier_semaphore()
    for who in ("partner", "plus", "minus", "deliver_a", "deliver_b"):
        pl.semaphore_signal(barrier, inc=1, device_id=here[who], device_id_type=MESH)

    @pl.when(gy > 0)
    def _():
        pl.semaphore_signal(barrier, inc=1, device_id=here["up"], device_id_type=MESH)

    @pl.when(gy < last_gy)
    def _():
        pl.semaphore_signal(barrier, inc=1, device_id=here["down"], device_id_type=MESH)

    @pl.when(gy == 0)
    def _():
        for _, vmem in arrays:
            vmem[:, :, 0:TOP, :] = jnp.zeros((4, NB, TOP, 128), jnp.float32)

    @pl.when(gy == last_gy)
    def _():
        for _, vmem in arrays:
            vmem[:, :, TOP + ROWS :, :] = jnp.zeros((4, NB, TOP, 128), jnp.float32)

    edges = jnp.where(gy > 0, 1, 0) + jnp.where(gy < last_gy, 1, 0)
    pl.semaphore_wait(barrier, 5 + edges)

    def remote(src, dst, send, recv, who):
        return pltpu.make_async_remote_copy(
            src_ref=src, dst_ref=dst, send_sem=send, recv_sem=recv,
            device_id=here[who], device_id_type=MESH,
        )

    pieces = (
        (0, TOP, ROWS, 0, 1),
        (0, TOP, ROWS, 1, 1),
        (0, TOP - MARGIN, MARGIN, 0, 2),
        (0, TOP + ROWS, MARGIN, 0, 2),
        (1, TOP - 2, ROWS + 4, 0, 2),
        (2, TOP - 1, ROWS + 2, 0, 2),
        (3, TOP, ROWS, 0, 1),
        (3, TOP, ROWS, 1, 1),
    )

    def near_copy(n, ref, stride):
        row = (TOP - MARGIN, TOP - 2, TOP - 1, TOP)[n]
        rows = ROWS + 2 * (TOP - row)
        return remote(
            ref.at[(1 - core) * stride, :, row : row + rows, :],
            got.at[core, n, :, row : row + rows, :], near_s.at[n], near_r.at[n], "partner",
        )

    def far_copy(j, ref, stride, way):
        n, row, rows, k, blocks = pieces[j]
        if ref is init:
            lanes = slice(128 * (2 * way + k), 128 * (2 * way + k + 1))
            src, dst = ref.at[core * stride, :, lanes], relay.at[n, way, k, row : row + rows, :]
        else:
            src = ref.at[core * stride, 2 * way + k : 2 * way + k + blocks, row : row + rows, :]
            dst = relay.at[n, way, k : k + blocks, row : row + rows, :]
        return remote(
            src, dst, far_s.at[j, way], hop_r.at[j, way], "minus" if way else "plus"
        )

    def hop_copy(j, way):
        n, row, rows, k, blocks = pieces[j]
        return remote(
            relay.at[n, way, k : k + blocks, row : row + rows, :],
            got.at[1 - core, n, 2 * way + k : 2 * way + k + blocks, row : row + rows, :],
            hop_s.at[j, way], far_r.at[j, way],
            "target_of_plus" if way else "target_of_minus",
        )

    sends = []

    def go(copy):
        copy.start()
        sends.append(copy)

    def send_far(js, ref, stride):
        for j in js:
            for way in range(2):
                go(far_copy(j, ref, stride, way))

    def relay_on(js):
        for j in js:
            for way in range(2):
                far_copy(j, u0, 3, way).wait_recv()
                go(hop_copy(j, way))

    def wait_faces(n):
        near_copy(n, u0, 3).wait_recv()
        for j in range(len(pieces)):
            if pieces[j][0] == n:
                for way in range(2):
                    hop_copy(j, way).wait_recv()

    def edge_copies(down):
        for i, (_, vmem) in enumerate(arrays):
            rows = MARGIN if i == 0 else MARGIN - 1
            taken = TOP + ROWS - rows if down else TOP
            put = TOP - rows if down else TOP + ROWS
            yield remote(
                vmem.at[:, :, taken : taken + rows, :], vmem.at[:, :, put : put + rows, :],
                edge_s.at[down, i], edge_r.at[down, i], "down" if down else "up",
            )

    for copy in loads:
        copy.wait()

    @pl.when(gy > 0)
    def _():
        for copy in edge_copies(0):
            copy.start()

    @pl.when(gy < last_gy)
    def _():
        for copy in edge_copies(1):
            copy.start()

    def take_edges():
        @pl.when(gy > 0)
        def _():
            for copy in edge_copies(1):
                copy.wait_recv()

        @pl.when(gy < last_gy)
        def _():
            for copy in edge_copies(0):
                copy.wait_recv()

    send_far((0, 1), u0, 3)

    lane = lax.broadcasted_iota(jnp.int32, (NB, 8, 128), 2)
    at_first, at_last = lane == 0, lane == 127
    zero = jnp.zeros((1, 8, 128), jnp.float32)

    def step(planes, which, dest, tiles, first, data=None, fresh=False):
        def tile(row):
            here_rows = pl.ds(row, 8)

            def read(p, shift=0):
                ref, i = planes[p]
                return ref[i, :, pl.ds(row + shift, 8), :]

            need = sorted({q for p in which for q in (p - 1, p, p + 1) if 0 <= q < 4})
            cells = {p: read(p) for p in need}

            def ghost(side, face):
                if data is None:
                    return face * FACE_W
                return face * FACE_W + got[side, data, :, here_rows, :] * DATA_W

            results = []
            for p in which:
                c = cells[p]
                minus_x = cells[p - 1] if p > 0 else ghost(0, c)
                plus_x = cells[p + 1] if p < 3 else ghost(1, c)
                ahead, behind = pltpu.roll(c, 127, 2), pltpu.roll(c, 1, 2)
                plus_z = jnp.where(at_last, jnp.concatenate([ahead[1:], zero], 0), ahead)
                minus_z = jnp.where(at_first, jnp.concatenate([zero, behind[:-1]], 0), behind)
                total = (plus_x + minus_x) + (read(p, 1) + read(p, -1)) + (plus_z + minus_z)
                k = kb[p, :, here_rows, :]
                v = vb[p, :, here_rows, :]
                q = rb[p, :, here_rows, :]
                a = (1.0 - 6.0 * k) - (v + q) if fresh else ab[p, :, here_rows, :]
                inner = a + q * pl.reciprocal(1.0 + c * c)
                results.append((p, a, c * inner + (k * total + v * minus_x)))
            return results

        def store(row, results):
            for p, a, value in results:
                if fresh:
                    ab[p, :, pl.ds(row, 8), :] = a
                if dest is None:
                    for k in range(NB):
                        out[p, pl.ds(row - TOP, 8), 128 * k : 128 * (k + 1)] = value[k]
                else:
                    ref, i = dest[p]
                    ref[i, :, pl.ds(row, 8), :] = value

        begin, end = tiles
        pairs = (end - begin) // 2

        def body(t, carry):
            row = pl.multiple_of(t * 16, 16) + (first + 8 * begin)
            one, two = tile(row), tile(row + 8)
            store(row, one)
            store(row + 8, two)
            return carry

        if pairs > 1:
            lax.fori_loop(0, pairs, body, 0)
        elif pairs:
            body(0, 0)
        if (end - begin) % 2:
            row = first + 8 * (end - 1)
            store(row, tile(row))

    def whole(ref):
        return [(ref, p) for p in range(4)]

    a0, a1, a2 = whole(u0), whole(u1), whole(u2)
    a3 = {0: (u3, 0), 3: (u3, 1)}
    b1 = [(v1, 0), (u1, 1), (u1, 2), (v1, 1)]
    b2, b3 = whole(v2), whole(v3)
    outer, inner = (0, 3), (1, 2)
    wide = ((0, 17), TOP - MARGIN)
    plain = ((0, 16), TOP)

    for which in (outer, inner):
        step(a0, which, a1, (1, 15), TOP - MARGIN, fresh=True)
    relay_on((0, 1))
    take_edges()
    for tiles in ((0, 1), (15, 17)):
        step(a0, outer, a1, tiles, TOP - MARGIN, fresh=True)
    send_far((4,), u1, 3)
    send_far((2, 3), u0, 3)
    go(near_copy(0, u0, 3))
    go(near_copy(1, u1, 3))
    for tiles in ((0, 1), (15, 17)):
        step(a0, inner, a1, tiles, TOP - MARGIN, fresh=True)
    step(a1, outer, a2, *wide)
    send_far((5,), u2, 3)
    go(near_copy(2, u2, 3))
    step(a1, inner, a2, *wide)
    step(a2, outer, a3, *plain)
    relay_on((4,))
    send_far((6, 7), u3, 1)
    go(near_copy(3, u3, 1))
    relay_on((2, 3))
    wait_faces(0)
    step(a0, outer, {0: b1[0], 3: b1[3]}, *wide, data=0)
    relay_on((5,))
    step(b1, inner, b2, *wide)
    relay_on((6, 7))
    wait_faces(1)
    step(b1, outer, b2, *wide, data=1)
    step(b2, inner, b3, *wide)
    wait_faces(2)
    step(b2, outer, b3, *wide, data=2)
    step(b3, inner, None, *plain)
    wait_faces(3)
    step(b3, outer, None, *plain, data=3)
    for copy in sends:
        copy.wait_send()

    @pl.when(gy > 0)
    def _():
        for copy in edge_copies(0):
            copy.wait_send()

    @pl.when(gy < last_gy)
    def _():
        for copy in edge_copies(1):
            copy.wait_send()


def local(initial, kappa, velocity, rate):
    tall = ROWS + 2 * TOP
    f32 = lambda *shape: pltpu.VMEM(shape, jnp.float32)
    full, pair = f32(4, NB, tall, 128), f32(2, NB, tall, 128)
    dma = pltpu.SemaphoreType.DMA
    return pl.pallas_call(
        kernel,
        out_shape=jax.ShapeDtypeStruct(initial.shape, jnp.float32),
        in_specs=[pl.BlockSpec(memory_space=pltpu.HBM)] * 4,
        out_specs=pl.BlockSpec(memory_space=pltpu.VMEM),
        scratch_shapes=[
            full, full, full, pair, pair, full, full,
            full, full, full, full,
            f32(2, STEPS, NB, tall, 128), f32(STEPS, 2, 2, tall, 128),
            dma((16,)), dma((STEPS,)), dma((STEPS,)),
            dma((8, 2)), dma((8, 2)), dma((8, 2)), dma((8, 2)),
            dma((2, 4)), dma((2, 4)),
        ],
        compiler_params=pltpu.CompilerParams(
            collective_id=0, has_side_effects=True, vmem_limit_bytes=40 * 2**20
        ),
        name="window",
    )(*(pltpu.with_memory_space_constraint(x, pltpu.HBM) for x in (initial, kappa, velocity, rate)))


def solution(mesh):
    placed = P("gx", "gy", None)
    return jax.shard_map(
        local, mesh=mesh, in_specs=(placed,) * 4, out_specs=placed, check_vma=False
    )
```
